128 devices in a mesh: grp: 4 (over z_hi, core), blk: 32 (over y, x, z_lo).
Axes of the slice: x: 4, y: 4, z: 4 (z_hi: 2, z_lo: 2; z = z_hi * 2 + z_lo), core: 2. Of those that a mesh axis runs over, the one named last changes fastest.
Arguments:
- targets: float32 [64, 262144], P('blk', 'grp'), may hold values from -6 to 6
- sources: float32 [128, 262144], P(('grp', 'blk')), may hold values from -6 to 6
- occupation: int32 [128], P(('grp', 'blk')), may hold values from 1 to 2
- offsets: int32 [4], replicated, may hold values from 0 to 31, as said below
Outputs:
- exchange: float32 [64, 262144], P('blk', 'grp')
The draws below stay inside these ranges and needn't reach their ends.
Inputs may be any that keep to these rules, and one draw needn't show every extreme that they name: The groups' offsets are distinct and the largest is 31.
All inputs are finite; a program needn't handle non-finite values.
Results may differ from the reference program's by a relative error of at most 0.0003.
Values sent between devices are 32-bit elements; how exact they have to be, the bound alone decides.
No kernel may reach another device: no remote copies, remote signals or barrier semaphores. Data moves between devices by JAX's collectives and lax.ppermute only.
A program may use at most 128 MiB of HBM per device.

```python
import math
import jax
import jax.numpy as jnp
from jax import lax

NG = 64
CELLS = 262144
TGT_DEV = 2
SRC_DEV = 1
STOPS = 4
GROUPS = 4
CYCLE = 32
TGT = 64
NSRC = 128


def draw_offsets(key, part):
    ordering = jax.random.permutation(key, jnp.arange(CYCLE, dtype=jnp.int32))[:GROUPS]
    return (ordering + (CYCLE - 1 - jnp.max(ordering))).astype(jnp.int32)


def plant(drawn, key, least, top_value):
    shape = drawn.shape
    place = [jax.random.randint(jax.random.fold_in(key, axis), (), 0, shape[axis]) for axis in range(len(shape))]
    drawn = drawn.at[tuple(place)].set(least)
    longest = shape.index(max(shape))
    place[longest] = (place[longest] + 1) % shape[longest]
    return drawn.at[tuple(place)].set(top_value)


def block_levels(own_key, shape, pieces, low, top_value):
    level, own = 1.0, jax.random.fold_in(own_key, 6)
    for axis_at, blocks in pieces:
        heights = jnp.exp(jax.random.uniform(jax.random.fold_in(own, axis_at), (blocks,), jnp.float32, low / len(pieces), top_value / len(pieces)))
        level = level * jnp.repeat(heights, shape[axis_at] // blocks).reshape([-1 if axis == axis_at else 1 for axis in range(len(shape))])
    return level


def centred(rng, dims, spread, bound, split=(), kind=jnp.bfloat16):
    array = spread * jax.random.normal(rng, dims, jnp.float32)
    if split:
        array = array * block_levels(rng, dims, split, -0.22, 0.18)
    return jnp.clip(array, -bound, bound).astype(kind)


def setup_inputs(seed: int = 0) -> dict:
    seeds = jax.random.split(jax.random.key(seed), 5)
    return {
        "targets": centred(seeds[0], (TGT, CELLS), 1.0, 6.0, ((0, 32), (1, 4)), jnp.float32),
        "sources": centred(seeds[1], (NSRC, CELLS), 1.0, 6.0, ((0, 128),), jnp.float32),
        "occupation": plant(jax.random.randint(seeds[2], (NSRC,), 1, 3), jax.random.fold_in(seeds[2], 1), 1, 2).astype(jnp.int32),
        "offsets": draw_offsets(jax.random.fold_in(seeds[4], 71), 0),
    }


box_length = 16.0
screen_square = 0.25

def screened_kernel(grid_size):
    counter = jnp.arange(grid_size, dtype=jnp.int32)
    signed_freq = jnp.where(counter < grid_size // 2, counter, counter - grid_size).astype(jnp.float32)
    wave_number = 2.0 * math.pi * signed_freq / box_length
    wave_square = wave_number * wave_number
    summed = wave_square[:, None, None] + wave_square[None, :, None] + wave_square[None, None, :]
    return 4.0 * math.pi / (summed + screen_square)

def pair_potential(density, kernel_grid):
    lead_shape = density.shape[:-1]
    cube_field = density.reshape(lead_shape + (NG, NG, NG))
    spectrum = jnp.fft.fftn(cube_field, axes=(-3, -2, -1))
    potential = jnp.real(jnp.fft.ifftn(spectrum * kernel_grid, axes=(-3, -2, -1)))
    return potential.astype(jnp.float32).reshape(lead_shape + (CELLS,))

def reference(targets, sources, occupation, offsets):
    scaled = sources * jnp.sqrt(occupation.astype(jnp.float32) * 0.5)[:, None]
    by_block = scaled.reshape(GROUPS, CYCLE, SRC_DEV, CELLS)
    target_blocks = targets.reshape(CYCLE, TGT_DEV, CELLS)
    kernel_grid = screened_kernel(NG)

    def one_block(inputs):
        block_index, target_rows = inputs
        accumulated = jnp.zeros((TGT_DEV, CELLS), jnp.float32)
        for group_index in range(GROUPS):
            for stop_index in range(STOPS):
                source_block = ((block_index - offsets[group_index] - stop_index) % CYCLE).astype(jnp.int32)
                partners = lax.dynamic_index_in_dim(by_block[group_index], source_block, 0, keepdims=False)
                density = target_rows[:, None, :] * partners[None, :, :]
                potential = pair_potential(density, kernel_grid)
                accumulated = accumulated + lax.optimization_barrier(jnp.sum(potential * partners[None, :, :], axis=1))
        return -accumulated
    result = lax.map(one_block, (jnp.arange(CYCLE, dtype=jnp.int32), target_blocks))
    return result.reshape(CYCLE * TGT_DEV, CELLS)
```

```python
import functools
import math

import jax
import jax.numpy as jnp
import numpy as np
from jax import lax
from jax.experimental import pallas as pl
from jax.experimental.pallas import tpu as pltpu
from jax.sharding import PartitionSpec as P

NG = 64
LANES = 128
ROWS = NG * NG
HALF = NG // 2
QUARTER = NG // 4
UNROLL = 32

box_length = 16.0
screen_square = 0.25
f32 = jnp.float32
bf16 = jnp.bfloat16


def two_terms(matrix):
    matrix = np.asarray(matrix, np.float32)
    high = matrix.astype(jnp.bfloat16)
    low = (matrix - high.astype(np.float32)).astype(jnp.bfloat16)
    return high, low


def tables():
    count = np.arange(NG)
    angle = 2.0 * np.pi * (count[:, None] * count[None, :] % NG) / NG
    h = np.cos(angle) + np.sin(angle)
    order = np.concatenate([np.arange(0, NG, 2), np.arange(1, NG, 2)])

    def left(matrix):
        high, low = two_terms(matrix)
        return np.concatenate([np.concatenate([high, high], 1), np.concatenate([low, low], 1)], 0)

    high, low = two_terms(np.kron(np.eye(2), h))
    right = np.concatenate([np.concatenate([high, low], 1)] * 2, 0)
    return left(h[:, order]), left(h), left(h[order, :]), right


def kernel_table():
    counter = jnp.arange(NG, dtype=jnp.int32)
    signed = jnp.where(counter < NG // 2, counter, counter - NG).astype(f32)
    wave = 2.0 * math.pi * signed / box_length
    square = wave * wave
    summed = square[:, None, None] + square[None, :, None] + jnp.concatenate([square, square])[None, None, :]
    return (4.0 * math.pi / NG**3 / (summed + screen_square)).reshape(ROWS, LANES)


def split(value):
    high = value.astype(bf16)
    low = (value - high.astype(f32)).astype(bf16)
    return high, low


def left_product(table, value):
    high, low = split(value)
    out = jnp.dot(table, jnp.concatenate([high, low], 0), preferred_element_type=f32)
    return out[:NG] + out[NG:]


def right_product(value, table):
    high, low = split(value)
    out = jnp.dot(jnp.concatenate([high, low], 1), table, preferred_element_type=f32)
    return out[:, :LANES] + out[:, LANES:]


def swap_pairs(first, second):
    low = lax.broadcasted_iota(jnp.int32, first.shape, 1) < NG
    return (
        jnp.where(low, first, pltpu.roll(second, NG, 1)),
        jnp.where(low, pltpu.roll(first, NG, 1), second),
    )


def spread(row):
    turned = pltpu.roll(row, NG, 1)
    low = lax.broadcasted_iota(jnp.int32, row.shape, 1) < NG
    return jnp.concatenate([jnp.where(low, row, turned), jnp.where(low, turned, row)], 0)


def halves(value, index):
    return value[:, LANES * index : LANES * index + LANES]


def stop_body(first, place, fields, row, weight, fwd_y, both_x, inv_y, both_z, *rest):
    if first:
        out, one, two = rest
        before = None
    else:
        before, out, one, two = rest

    def position(step, u):
        return place[step * (UNROLL // QUARTER) + u // QUARTER] + u % QUARTER

    def row_at(x):
        return spread(row[pl.ds(pl.multiple_of(x * HALF, HALF), HALF), :])

    @pl.loop(0, NG // UNROLL)
    def _(step):
        products = []
        for u in range(UNROLL):
            density = fields[pl.ds((step * UNROLL + u) * NG, NG), :] * row_at(position(step, u))
            products.append(density)
        moved = [
            left_product(fwd_y[...], jnp.concatenate(products[u : u + 2], 1)) for u in range(0, UNROLL, 2)
        ]
        for u in range(UNROLL):
            one[pl.ds(position(step, u), NG, NG), :] = halves(moved[u // 2], u % 2)

    @pl.loop(0, NG // UNROLL)
    def _(step):
        moved = []
        for u in range(0, UNROLL, 2):
            k = step * UNROLL + u
            pair = jnp.concatenate([one[pl.ds(k * NG, NG), :], one[pl.ds((k + 1) * NG, NG), :]], 1)
            pair = left_product(both_x[...], pair)
            moved += [halves(pair, 0), halves(pair, 1)]
        plane = right_product(jnp.concatenate(moved, 0), both_z[...])
        plane = plane * weight[pl.ds(step * UNROLL * NG, UNROLL * NG), :]
        plane = right_product(plane, both_z[...])
        for u in range(0, UNROLL, 2):
            k = step * UNROLL + u
            pair = jnp.concatenate([plane[u * NG : (u + 1) * NG], plane[(u + 1) * NG : (u + 2) * NG]], 1)
            pair = left_product(both_x[...], pair)
            two[pl.ds(k, NG, NG), :] = halves(pair, 0)
            two[pl.ds(k + 1, NG, NG), :] = halves(pair, 1)

    @pl.loop(0, NG // UNROLL)
    def _(step):
        moved = []
        for u in range(0, UNROLL, 2):
            planes = [
                two[pl.ds(pl.multiple_of(position(step, v) * NG, NG), NG), :] for v in (u, u + 1)
            ]
            moved.append(left_product(inv_y[...], jnp.concatenate(planes, 1)))
        for u in range(UNROLL):
            value = halves(moved[u // 2], u % 2) * row_at(position(step, u))
            at = pl.ds((step * UNROLL + u) * NG, NG)
            if before is not None:
                value = value + before[at, :]
            out[at, :] = value


def stop(place, fields, row, weight, constants, before):
    vmem = pl.BlockSpec(memory_space=pltpu.VMEM)
    args = [place, fields, row, weight, *constants] + ([] if before is None else [before])
    return pl.pallas_call(
        functools.partial(stop_body, before is None),
        out_shape=jax.ShapeDtypeStruct((ROWS, LANES), f32),
        in_specs=[pl.BlockSpec(memory_space=pltpu.SMEM)] + [vmem] * (len(args) - 1),
        out_specs=vmem,
        scratch_shapes=[pltpu.VMEM((ROWS, LANES), f32), pltpu.VMEM((ROWS, LANES), f32)],
        compiler_params=pltpu.CompilerParams(vmem_limit_bytes=40 * 2**20),
        name="stop",
    )(*args)


def arrange_body(rows, out):
    for x in range(QUARTER):
        pair = [rows[pl.ds(x * NG + t, HALF, 2), :] for t in range(2)]
        even, odd = swap_pairs(*pair)
        out[x * NG : x * NG + HALF, :] = even
        out[x * NG + HALF : (x + 1) * NG, :] = odd


def finish_body(mine, other, out):
    for x in range(QUARTER):
        part = -(mine[x * NG : (x + 1) * NG, :] + other[x * NG : (x + 1) * NG, :])
        for t, value in enumerate(swap_pairs(part[:HALF], part[HALF:])):
            out[pl.ds(x * NG + t, HALF, 2), :] = value


def small(body, *args, name):
    return pl.pallas_call(body, out_shape=jax.ShapeDtypeStruct((ROWS // 4, LANES), f32), name=name)(*args)


def moved(block, axes, route):
    return lax.ppermute(block, axes, route)


def everywhere(block, target):
    route = [(g * 32 + b, (lambda to: to[0] * 32 + to[1])(target(g, b))) for g in range(4) for b in range(32)]
    return lax.ppermute(block, ("grp", "blk"), route)


def pair_shift(block, distance):
    if distance % 16 == 0:
        return block
    return lax.ppermute(block, "blk", [(b, (b + 2 * distance) % 32) for b in range(32)])


def local(targets, sources, occupation, offsets):
    group = lax.axis_index("grp")
    low_z = lax.axis_index("blk") % 2

    rows = targets.reshape(2, 512, LANES).transpose(1, 0, 2).reshape(1024, LANES)
    mine = small(arrange_body, rows, name="arrange")
    far = everywhere(mine, lambda g, b: (g ^ 2, b))
    near = everywhere(jnp.concatenate([mine, far], 0), lambda g, b: (g ^ 1, b))
    fields = jnp.concatenate([mine, far, near], 0)
    place = (group ^ jnp.array([0, 2, 1, 3], jnp.int32)) * QUARTER

    scaled = sources * jnp.sqrt(occupation.astype(f32) * 0.5)[:, None]
    scaled = scaled.reshape(ROWS // 2, LANES)
    offset = lax.dynamic_index_in_dim(offsets, group, 0, keepdims=False)
    own = lax.switch(
        (offset // 2 + 1) % 16, [functools.partial(pair_shift, distance=d) for d in range(16)], scaled
    )

    def cross(block):
        return everywhere(block, lambda g, b: (g ^ 2 if g % 2 else g, b ^ 1))

    crossed = cross(own)
    after = pair_shift(own, 1)
    ahead = pair_shift(own, 15)
    same = jnp.where(offset % 2 == 0, ahead, after)
    last = cross(jnp.where(low_z == 1, after, ahead))

    weight = kernel_table()
    constants = [jnp.asarray(table) for table in tables()]
    total = None
    for row in (own, crossed, same, last):
        total = stop(place, fields, row, weight, constants, total)

    partner = everywhere(total[2048:], lambda g, b: (g ^ 1, b))
    total = total[:2048] + partner
    other = everywhere(total[1024:], lambda g, b: (g ^ 2, b))
    result = small(finish_body, total[:1024], other, name="finish")
    return result.reshape(512, 2, LANES).transpose(1, 0, 2).reshape(2, 65536)


def solution(mesh):
    in_specs = (P("blk", "grp"), P(("grp", "blk"), None), P(("grp", "blk")), P())
    out_specs = P("blk", "grp")
    return jax.shard_map(local, mesh=mesh, in_specs=in_specs, out_specs=out_specs, check_vma=False)
```

```python
import functools
import math

import jax
import jax.numpy as jnp
import numpy as np
from jax import lax
from jax.experimental import pallas as pl
from jax.experimental.pallas import tpu as pltpu
from jax.sharding import PartitionSpec as P

NG = 64
LANES = 128
ROWS = NG * NG
HALF = NG // 2
QUARTER = NG // 4
UNROLL = 32
STRIDE = 72

box_length = 16.0
screen_square = 0.25
f32 = jnp.float32
bf16 = jnp.bfloat16


def two_terms(matrix):
    matrix = np.asarray(matrix, np.float32)
    high = matrix.astype(jnp.bfloat16)
    low = (matrix - high.astype(np.float32)).astype(jnp.bfloat16)
    return high, low


def tables():
    count = np.arange(NG)
    angle = 2.0 * np.pi * (count[:, None] * count[None, :] % NG) / NG
    h = np.cos(angle) + np.sin(angle)
    order = np.concatenate([np.arange(0, NG, 2), np.arange(1, NG, 2)])

    def left(matrix):
        high, low = two_terms(matrix)
        return np.concatenate([np.concatenate([high, high], 1), np.concatenate([low, low], 1)], 0)

    high, low = two_terms(np.kron(np.eye(2), h))
    right = np.concatenate([np.concatenate([high, low], 1)] * 2, 0)
    return left(h[:, order]), left(h), left(h[order, :]), right


def kernel_table():
    counter = jnp.arange(NG, dtype=jnp.int32)
    signed = jnp.where(counter < NG // 2, counter, counter - NG).astype(f32)
    wave = 2.0 * math.pi * signed / box_length
    square = wave * wave
    summed = square[:, None, None] + square[None, :, None] + jnp.concatenate([square, square])[None, None, :]
    return (4.0 * math.pi / NG**3 / (summed + screen_square)).reshape(ROWS, LANES)


def split(value):
    high = value.astype(bf16)
    low = (value - high.astype(f32)).astype(bf16)
    return high, low


def left_product(table, value):
    high, low = split(value)
    out = jnp.dot(table, jnp.concatenate([high, low], 0), preferred_element_type=f32)
    return out[:NG] + out[NG:]


def right_product(value, table):
    high, low = split(value)
    out = jnp.dot(jnp.concatenate([high, low], 1), table, preferred_element_type=f32)
    return out[:, :LANES] + out[:, LANES:]


def swap_pairs(first, second):
    low = lax.broadcasted_iota(jnp.int32, first.shape, 1) < NG
    return (
        jnp.where(low, first, pltpu.roll(second, NG, 1)),
        jnp.where(low, pltpu.roll(first, NG, 1), second),
    )


def spread(row):
    turned = pltpu.roll(row, NG, 1)
    low = lax.broadcasted_iota(jnp.int32, row.shape, 1) < NG
    return jnp.concatenate([jnp.where(low, row, turned), jnp.where(low, turned, row)], 0)


def halves(value, index):
    return value[:, LANES * index : LANES * index + LANES]


TURNS = (0, 2, 1, 3)


def whole_rows(x, count):
    return pl.ds(pl.multiple_of(x * count, 8), count)


def stop_body(first, final, place, weight, fwd_y, both_x, inv_y, both_z, row, *rest):
    fields, rest = rest[:4], rest[4:]
    if not first:
        before, rest = rest[0], rest[1:]
    out, (one, two) = rest[:-2], rest[-2:]

    def part(x):
        return spread(row[whole_rows(x, HALF), :])

    for turns in (TURNS[:2], TURNS[2:]):
        where = [(turn, u, (place[0] ^ turn) * QUARTER + u) for turn in turns for u in range(QUARTER)]
        products = []
        for turn, u, x in where:
            pair = swap_pairs(*[fields[turn][pl.ds(u * NG + t, HALF, 2), :] for t in range(2)])
            products.append(jnp.concatenate(pair, 0) * part(x))
        moved = [
            left_product(fwd_y[...], jnp.concatenate(products[i : i + 2], 1)) for i in range(0, len(where), 2)
        ]
        for i, (_, _, x) in enumerate(where):
            one[pl.ds(x, NG, STRIDE), :] = halves(moved[i // 2], i % 2)

    for start in range(0, NG, UNROLL):
        moved = []
        for k in range(start, start + UNROLL, 2):
            pair = jnp.concatenate([one[v * STRIDE : v * STRIDE + NG, :] for v in (k, k + 1)], 1)
            pair = left_product(both_x[...], pair)
            moved += [halves(pair, 0), halves(pair, 1)]
        plane = right_product(jnp.concatenate(moved, 0), both_z[...])
        plane = plane * weight[start * NG : (start + UNROLL) * NG, :]
        plane = right_product(plane, both_z[...])
        for u in range(0, UNROLL, 2):
            pair = jnp.concatenate([plane[v * NG : (v + 1) * NG] for v in (u, u + 1)], 1)
            pair = left_product(both_x[...], pair)
            for v in range(2):
                two[pl.ds(start + u + v, NG, STRIDE), :] = halves(pair, v)

    for step, turns in enumerate(((1, 3), (0, 2))):
        if final:
            where = [(place[0] ^ turn) * QUARTER + u for turn in turns for u in range(QUARTER)]
        else:
            where = list(range(step * HALF, (step + 1) * HALF))
        moved = []
        for i in range(0, HALF, 2):
            planes = [two[pl.ds(pl.multiple_of(x * STRIDE, 8), NG), :] for x in where[i : i + 2]]
            moved.append(left_product(inv_y[...], jnp.concatenate(planes, 1)))
        for i, x in enumerate(where):
            value = halves(moved[i // 2], i % 2) * part(x)
            if not first:
                value = value + before[whole_rows(x, NG), :]
            if final:
                for t, field in enumerate(swap_pairs(value[:HALF], value[HALF:])):
                    out[step][pl.ds(i * NG + t, HALF, 2), :] = field
            else:
                out[0][whole_rows(x, NG), :] = value


def stop(place, weight, constants, fields, row, before=None, final=False):
    vmem = pl.BlockSpec(memory_space=pltpu.VMEM)
    args = [place, weight, *constants, row, *fields] + ([] if before is None else [before])
    half = jax.ShapeDtypeStruct((ROWS // 2, LANES), f32)
    return pl.pallas_call(
        functools.partial(stop_body, before is None, final),
        out_shape=(half, half) if final else jax.ShapeDtypeStruct((ROWS, LANES), f32),
        in_specs=[pl.BlockSpec(memory_space=pltpu.SMEM)] + [vmem] * (len(args) - 1),
        out_specs=(vmem, vmem) if final else vmem,
        scratch_shapes=[pltpu.VMEM((NG * STRIDE, LANES), f32)] * 2,
        compiler_params=pltpu.CompilerParams(vmem_limit_bytes=40 * 2**20),
        name="stop",
    )(*args)


def moved(block, axes, route):
    return lax.ppermute(block, axes, route)


def everywhere(block, target):
    route = [(g * 32 + b, (lambda to: to[0] * 32 + to[1])(target(g, b))) for g in range(4) for b in range(32)]
    return lax.ppermute(block, ("grp", "blk"), route)


def pair_shift(block, distance):
    if distance % 16 == 0:
        return block
    return lax.ppermute(block, "blk", [(b, (b + 2 * distance) % 32) for b in range(32)])


def local(targets, sources, occupation, offsets):
    group = lax.axis_index("grp")
    low_z = lax.axis_index("blk") & 1

    rows = targets.reshape(2, 512, LANES).transpose(1, 0, 2).reshape(1024, LANES)
    fields = [everywhere(rows, lambda g, b, turn=turn: (g ^ turn, b)) for turn in (1, 2, 3)]

    scaled = (sources * jnp.sqrt(occupation.astype(f32) * 0.5)[:, None]).reshape(ROWS // 2, LANES)
    offset = lax.dynamic_index_in_dim(offsets, group, 0, keepdims=False)
    own = lax.switch(
        (lax.shift_right_logical(offset, 1) + 1) & 15,
        [functools.partial(pair_shift, distance=d) for d in range(16)],
        scaled,
    )
    own, *fields = lax.optimization_barrier((own, *fields))

    def cross(block):
        return everywhere(block, lambda g, b: (g ^ 2 if g % 2 else g, b ^ 1))

    def beside(block, sign):
        return lax.ppermute(block, "blk", [(b, (b + (2 if b & 1 else -2) * sign) % 32) for b in range(32)])

    weight = kernel_table()
    constants = [jnp.asarray(table) for table in tables()]
    common = (group.reshape(1).astype(jnp.int32), weight, constants, [rows, *fields])

    crossed = cross(own)
    side = beside(own, 1)
    other_side = beside(own, -1)
    total = stop(*common, own)
    total = stop(*common, crossed, total)
    total, side = lax.optimization_barrier((total, side))
    last = cross(side)
    same = jnp.where(((offset + low_z) & 1) == 0, side, other_side)
    total = stop(*common, same, total)
    send, keep = stop(*common, last, total, True)

    near = everywhere(send, lambda g, b: (g ^ 1, b))
    far = everywhere(keep[1024:] + near[1024:], lambda g, b: (g ^ 2, b))
    result = -(keep[:1024] + near[:1024] + far)
    return result.reshape(512, 2, LANES).transpose(1, 0, 2).reshape(2, 65536)


def solution(mesh):
    in_specs = (P("blk", "grp"), P(("grp", "blk"), None), P(("grp", "blk")), P())
    out_specs = P("blk", "grp")
    return jax.shard_map(local, mesh=mesh, in_specs=in_specs, out_specs=out_specs, check_vma=False)
```

```python
import functools
import math

import jax
import jax.numpy as jnp
import numpy as np
from jax import lax
from jax.experimental import pallas as pl
from jax.experimental.pallas import tpu as pltpu
from jax.sharding import PartitionSpec as P

NG = 64
LANES = 128
ROWS = NG * NG
HALF = NG // 2
QUARTER = NG // 4
UNROLL = 32
FLOPS = 20_000_000_000
STRIDE = 72

box_length = 16.0
screen_square = 0.25
f32 = jnp.float32
bf16 = jnp.bfloat16


def two_terms(matrix):
    matrix = np.asarray(matrix, np.float32)
    high = matrix.astype(jnp.bfloat16)
    low = (matrix - high.astype(np.float32)).astype(jnp.bfloat16)
    return high, low


def tables():
    count = np.arange(NG)
    angle = 2.0 * np.pi * (count[:, None] * count[None, :] % NG) / NG
    h = np.cos(angle) + np.sin(angle)
    order = np.concatenate([np.arange(0, NG, 2), np.arange(1, NG, 2)])

    def left(matrix):
        high, low = two_terms(matrix)
        return np.concatenate([np.concatenate([high, high], 1), np.concatenate([low, low], 1)], 0)

    high, low = two_terms(np.kron(np.eye(2), h))
    right = np.concatenate([np.concatenate([high, low], 1)] * 2, 0)
    return left(h[:, order]), left(h), left(h[order, :]), right


def kernel_table():
    counter = jnp.arange(NG, dtype=jnp.int32)
    signed = jnp.where(counter < NG // 2, counter, counter - NG).astype(f32)
    wave = 2.0 * math.pi * signed / box_length
    square = wave * wave
    summed = square[:, None, None] + square[None, :, None] + jnp.concatenate([square, square])[None, None, :]
    return (4.0 * math.pi / NG**3 / (summed + screen_square)).reshape(ROWS, LANES)


def split(value):
    high = value.astype(bf16)
    low = (value - high.astype(f32)).astype(bf16)
    return high, low


def left_product(table, value):
    high, low = split(value)
    out = jnp.dot(table, jnp.concatenate([high, low], 0), preferred_element_type=f32)
    return out[:NG] + out[NG:]


def right_product(value, table):
    high, low = split(value)
    out = jnp.dot(jnp.concatenate([high, low], 1), table, preferred_element_type=f32)
    return out[:, :LANES] + out[:, LANES:]


def swap_pairs(first, second):
    low = lax.broadcasted_iota(jnp.int32, first.shape, 1) < NG
    return (
        jnp.where(low, first, pltpu.roll(second, NG, 1)),
        jnp.where(low, pltpu.roll(first, NG, 1), second),
    )


def spread(row):
    turned = pltpu.roll(row, NG, 1)
    low = lax.broadcasted_iota(jnp.int32, row.shape, 1) < NG
    return jnp.concatenate([jnp.where(low, row, turned), jnp.where(low, turned, row)], 0)


def halves(value, index):
    return value[:, LANES * index : LANES * index + LANES]


TURNS = (0, 2, 1, 3)


def whole_rows(x, count):
    return pl.ds(pl.multiple_of(x * count, 8), count)


def stop_body(first, final, place, weight, fwd_y, both_x, inv_y, both_z, row, *rest):
    fields, rest = rest[:4], rest[4:]
    if not first:
        before, rest = rest[0], rest[1:]
    out, (one, two) = rest[:-2], rest[-2:]

    def part(x):
        return spread(row[whole_rows(x, HALF), :])

    for turns in (TURNS[:2], TURNS[2:]):
        where = [(turn, u, (place[0] ^ turn) * QUARTER + u) for turn in turns for u in range(QUARTER)]
        products = []
        for turn, u, x in where:
            pair = swap_pairs(*[fields[turn][pl.ds(u * NG + t, HALF, 2), :] for t in range(2)])
            products.append(jnp.concatenate(pair, 0) * part(x))
        moved = [
            left_product(fwd_y[...], jnp.concatenate(products[i : i + 2], 1)) for i in range(0, len(where), 2)
        ]
        for i, (_, _, x) in enumerate(where):
            one[pl.ds(x, NG, STRIDE), :] = halves(moved[i // 2], i % 2)

    for start in range(0, NG, UNROLL):
        moved = []
        for k in range(start, start + UNROLL, 2):
            pair = jnp.concatenate([one[v * STRIDE : v * STRIDE + NG, :] for v in (k, k + 1)], 1)
            pair = left_product(both_x[...], pair)
            moved += [halves(pair, 0), halves(pair, 1)]
        plane = right_product(jnp.concatenate(moved, 0), both_z[...])
        plane = plane * weight[start * NG : (start + UNROLL) * NG, :]
        plane = right_product(plane, both_z[...])
        for u in range(0, UNROLL, 2):
            pair = jnp.concatenate([plane[v * NG : (v + 1) * NG] for v in (u, u + 1)], 1)
            pair = left_product(both_x[...], pair)
            for v in range(2):
                two[pl.ds(start + u + v, NG, STRIDE), :] = halves(pair, v)

    for step, turns in enumerate(((1, 3), (0, 2))):
        if final:
            where = [(place[0] ^ turn) * QUARTER + u for turn in turns for u in range(QUARTER)]
        else:
            where = list(range(step * HALF, (step + 1) * HALF))
        moved = []
        for i in range(0, HALF, 2):
            planes = [two[pl.ds(pl.multiple_of(x * STRIDE, 8), NG), :] for x in where[i : i + 2]]
            moved.append(left_product(inv_y[...], jnp.concatenate(planes, 1)))
        for i, x in enumerate(where):
            value = halves(moved[i // 2], i % 2) * part(x)
            if not first:
                value = value + before[whole_rows(x, NG), :]
            if final:
                for t, field in enumerate(swap_pairs(value[:HALF], value[HALF:])):
                    out[step][pl.ds(i * NG + t, HALF, 2), :] = field
            else:
                out[0][whole_rows(x, NG), :] = value


def stop(place, weight, constants, fields, row, before=None, final=False):
    vmem = pl.BlockSpec(memory_space=pltpu.VMEM)
    args = [place, weight, *constants, row, *fields] + ([] if before is None else [before])
    half = jax.ShapeDtypeStruct((ROWS // 2, LANES), f32)
    return pl.pallas_call(
        functools.partial(stop_body, before is None, final),
        out_shape=(half, half) if final else jax.ShapeDtypeStruct((ROWS, LANES), f32),
        in_specs=[pl.BlockSpec(memory_space=pltpu.SMEM)] + [vmem] * (len(args) - 1),
        out_specs=(vmem, vmem) if final else vmem,
        scratch_shapes=[pltpu.VMEM((NG * STRIDE, LANES), f32)] * 2,
        compiler_params=pltpu.CompilerParams(vmem_limit_bytes=16 * 2**20),
        cost_estimate=pl.CostEstimate(flops=FLOPS, bytes_accessed=9 * 2**20, transcendentals=0),
        name="stop",
    )(*args)


def moved(block, axes, route):
    return lax.ppermute(block, axes, route)


def everywhere(block, target):
    route = [(g * 32 + b, (lambda to: to[0] * 32 + to[1])(target(g, b))) for g in range(4) for b in range(32)]
    return lax.ppermute(block, ("grp", "blk"), route)


def pair_shift(block, distance):
    if distance % 16 == 0:
        return block
    return lax.ppermute(block, "blk", [(b, (b + 2 * distance) % 32) for b in range(32)])


def local(targets, sources, occupation, offsets):
    group = lax.axis_index("grp")
    low_z = lax.axis_index("blk") & 1

    rows = targets.reshape(2, 512, LANES).transpose(1, 0, 2).reshape(1024, LANES)
    fields = [everywhere(rows, lambda g, b, turn=turn: (g ^ turn, b)) for turn in (1, 2, 3)]

    scaled = (sources * jnp.sqrt(occupation.astype(f32) * 0.5)[:, None]).reshape(ROWS // 2, LANES)
    offset = lax.dynamic_index_in_dim(offsets, group, 0, keepdims=False)
    own = lax.switch(
        (lax.shift_right_logical(offset, 1) + 1) & 15,
        [functools.partial(pair_shift, distance=d) for d in range(16)],
        scaled,
    )
    own, *fields = lax.optimization_barrier((own, *fields))

    def cross(block):
        return everywhere(block, lambda g, b: (g ^ 2 if g % 2 else g, b ^ 1))

    def beside(block, sign):
        return lax.ppermute(block, "blk", [(b, (b + (2 if b & 1 else -2) * sign) % 32) for b in range(32)])

    weight = kernel_table()
    constants = [jnp.asarray(table) for table in tables()]
    common = (group.reshape(1).astype(jnp.int32), weight, constants, [rows, *fields])

    crossed = cross(own)
    side = beside(own, 1)
    other_side = beside(own, -1)
    total = stop(*common, own)
    total = stop(*common, crossed, total)
    last = cross(side)
    same = jnp.where(((offset + low_z) & 1) == 0, side, other_side)
    total = stop(*common, same, total)
    send, keep = stop(*common, last, total, True)

    near = everywhere(send, lambda g, b: (g ^ 1, b))
    far = everywhere(keep[1024:] + near[1024:], lambda g, b: (g ^ 2, b))
    result = -(keep[:1024] + near[:1024] + far)
    return result.reshape(512, 2, LANES).transpose(1, 0, 2).reshape(2, 65536)


def solution(mesh):
    in_specs = (P("blk", "grp"), P(("grp", "blk"), None), P(("grp", "blk")), P())
    out_specs = P("blk", "grp")
    return jax.shard_map(local, mesh=mesh, in_specs=in_specs, out_specs=out_specs, check_vma=False)
```

```python
import functools
import math

import jax
import jax.numpy as jnp
import numpy as np
from jax import lax
from jax.experimental import pallas as pl
from jax.experimental.pallas import tpu as pltpu
from jax.sharding import PartitionSpec as P

NG = 64
LANES = 128
ROWS = NG * NG
HALF = NG // 2
QUARTER = NG // 4
UNROLL = 32
FLOPS = 20_000_000_000
STRIDE = 72

box_length = 16.0
screen_square = 0.25
f32 = jnp.float32
bf16 = jnp.bfloat16


def two_terms(matrix):
    matrix = np.asarray(matrix, np.float32)
    high = matrix.astype(jnp.bfloat16)
    low = (matrix - high.astype(np.float32)).astype(jnp.bfloat16)
    return high, low


def tables():
    count = np.arange(NG)
    angle = 2.0 * np.pi * (count[:, None] * count[None, :] % NG) / NG
    h = np.cos(angle) + np.sin(angle)
    order = np.concatenate([np.arange(0, NG, 2), np.arange(1, NG, 2)])

    def left(matrix):
        high, low = two_terms(matrix)
        return np.concatenate([np.concatenate([high, high], 1), np.concatenate([low, low], 1)], 0)

    high, low = two_terms(np.kron(np.eye(2), h))
    right = np.concatenate([np.concatenate([high, low], 1)] * 2, 0)
    return left(h[:, order]), left(h), left(h[order, :]), right


def kernel_table():
    counter = jnp.arange(NG, dtype=jnp.int32)
    signed = jnp.where(counter < NG // 2, counter, counter - NG).astype(f32)
    wave = 2.0 * math.pi * signed / box_length
    square = wave * wave
    summed = square[:, None, None] + square[None, :, None] + jnp.concatenate([square, square])[None, None, :]
    return (4.0 * math.pi / NG**3 / (summed + screen_square)).reshape(ROWS, LANES)


def split(value):
    high = value.astype(bf16)
    low = (value - high.astype(f32)).astype(bf16)
    return high, low


def left_product(table, value):
    high, low = split(value)
    out = jnp.dot(table, jnp.concatenate([high, low], 0), preferred_element_type=f32)
    return out[:NG] + out[NG:]


def right_product(value, table):
    high, low = split(value)
    out = jnp.dot(jnp.concatenate([high, low], 1), table, preferred_element_type=f32)
    return out[:, :LANES] + out[:, LANES:]


def swap_pairs(first, second):
    low = lax.broadcasted_iota(jnp.int32, first.shape, 1) < NG
    return (
        jnp.where(low, first, pltpu.roll(second, NG, 1)),
        jnp.where(low, pltpu.roll(first, NG, 1), second),
    )


def spread(row):
    turned = pltpu.roll(row, NG, 1)
    low = lax.broadcasted_iota(jnp.int32, row.shape, 1) < NG
    return jnp.concatenate([jnp.where(low, row, turned), jnp.where(low, turned, row)], 0)


def halves(value, index):
    return value[:, LANES * index : LANES * index + LANES]


TURNS = (0, 2, 1, 3)


def whole_rows(x, count):
    return pl.ds(pl.multiple_of(x * count, 8), count)


def stop_body(chunks, first, final, place, weight, fwd_y, both_x, inv_y, both_z, *rest):
    row, rest = rest[:chunks], rest[chunks:]
    if chunks > 1:
        rest, whole = rest[:-1], rest[-1]
        size = ROWS // 2 // chunks
        for c in range(chunks):
            whole[c * size : (c + 1) * size, :] = row[c][...]
        row = whole
    else:
        row = row[0]
    fields, rest = rest[:4], rest[4:]
    if not first:
        before, rest = rest[0], rest[1:]
    out, (one, two) = rest[:-2], rest[-2:]

    def part(x):
        return spread(row[whole_rows(x, HALF), :])

    for turns in (TURNS[:2], TURNS[2:]):
        where = [(turn, u, (place[0] ^ turn) * QUARTER + u) for turn in turns for u in range(QUARTER)]
        products = []
        for turn, u, x in where:
            pair = swap_pairs(*[fields[turn][pl.ds(u * NG + t, HALF, 2), :] for t in range(2)])
            products.append(jnp.concatenate(pair, 0) * part(x))
        moved = [
            left_product(fwd_y[...], jnp.concatenate(products[i : i + 2], 1)) for i in range(0, len(where), 2)
        ]
        for i, (_, _, x) in enumerate(where):
            one[pl.ds(x, NG, STRIDE), :] = halves(moved[i // 2], i % 2)

    for start in range(0, NG, UNROLL):
        moved = []
        for k in range(start, start + UNROLL, 2):
            pair = jnp.concatenate([one[v * STRIDE : v * STRIDE + NG, :] for v in (k, k + 1)], 1)
            pair = left_product(both_x[...], pair)
            moved += [halves(pair, 0), halves(pair, 1)]
        plane = right_product(jnp.concatenate(moved, 0), both_z[...])
        plane = plane * weight[start * NG : (start + UNROLL) * NG, :]
        plane = right_product(plane, both_z[...])
        for u in range(0, UNROLL, 2):
            pair = jnp.concatenate([plane[v * NG : (v + 1) * NG] for v in (u, u + 1)], 1)
            pair = left_product(both_x[...], pair)
            for v in range(2):
                two[pl.ds(start + u + v, NG, STRIDE), :] = halves(pair, v)

    for step, turns in enumerate(((1, 3), (0, 2))):
        if final:
            where = [(place[0] ^ turn) * QUARTER + u for turn in turns for u in range(QUARTER)]
        else:
            where = list(range(step * HALF, (step + 1) * HALF))
        moved = []
        for i in range(0, HALF, 2):
            planes = [two[pl.ds(pl.multiple_of(x * STRIDE, 8), NG), :] for x in where[i : i + 2]]
            moved.append(left_product(inv_y[...], jnp.concatenate(planes, 1)))
        for i, x in enumerate(where):
            value = halves(moved[i // 2], i % 2) * part(x)
            if not first:
                value = value + before[whole_rows(x, NG), :]
            if final:
                for t, field in enumerate(swap_pairs(value[:HALF], value[HALF:])):
                    out[step][pl.ds(i * NG + t, HALF, 2), :] = field
            else:
                out[0][whole_rows(x, NG), :] = value


def stop(place, weight, constants, fields, row, before=None, final=False):
    vmem = pl.BlockSpec(memory_space=pltpu.VMEM)
    args = [place, weight, *constants, *row, *fields] + ([] if before is None else [before])
    half = jax.ShapeDtypeStruct((ROWS // 2, LANES), f32)
    return pl.pallas_call(
        functools.partial(stop_body, len(row), before is None, final),
        out_shape=(half, half) if final else jax.ShapeDtypeStruct((ROWS, LANES), f32),
        in_specs=[pl.BlockSpec(memory_space=pltpu.SMEM)] + [vmem] * (len(args) - 1),
        out_specs=(vmem, vmem) if final else vmem,
        scratch_shapes=[pltpu.VMEM((NG * STRIDE, LANES), f32)] * 2
        + [pltpu.VMEM((ROWS // 2, LANES), f32)] * (len(row) > 1),
        compiler_params=pltpu.CompilerParams(vmem_limit_bytes=16 * 2**20),
        cost_estimate=pl.CostEstimate(flops=FLOPS, bytes_accessed=9 * 2**20, transcendentals=0),
        name="stop",
    )(*args)


def scale_body(occupation, row, out):
    factor = jnp.sqrt(jnp.full((8, LANES), occupation[0], jnp.int32).astype(f32) * 0.5)
    for at in range(0, ROWS // 2, 8):
        out[at : at + 8, :] = row[at : at + 8, :] * factor


def moved(block, axes, route):
    return lax.ppermute(block, axes, route)


def everywhere(block, target):
    route = [(g * 32 + b, (lambda to: to[0] * 32 + to[1])(target(g, b))) for g in range(4) for b in range(32)]
    return lax.ppermute(block, ("grp", "blk"), route)


def pair_shift(block, distance):
    if distance % 16 == 0:
        return block
    return lax.ppermute(block, "blk", [(b, (b + 2 * distance) % 32) for b in range(32)])


def local(targets, sources, occupation, offsets):
    group = lax.axis_index("grp")
    low_z = lax.axis_index("blk") & 1

    rows = targets.reshape(2, 512, LANES).transpose(1, 0, 2).reshape(1024, LANES)
    fields = [everywhere(rows, lambda g, b, turn=turn: (g ^ turn, b)) for turn in (1, 2, 3)]

    scaled = pl.pallas_call(
        scale_body,
        out_shape=jax.ShapeDtypeStruct((ROWS // 2, LANES), f32),
        in_specs=[pl.BlockSpec(memory_space=pltpu.SMEM), pl.BlockSpec(memory_space=pltpu.VMEM)],
        name="scale",
    )(occupation, sources.reshape(ROWS // 2, LANES))
    offset = lax.dynamic_index_in_dim(offsets, group, 0, keepdims=False)
    own = lax.switch(
        (lax.shift_right_logical(offset, 1) + 1) & 15,
        [functools.partial(pair_shift, distance=d) for d in range(16)],
        scaled,
    )
    own, *fields = lax.optimization_barrier((own, *fields))

    def cross(block):
        return everywhere(block, lambda g, b: (g ^ 2 if g % 2 else g, b ^ 1))

    def beside(block, sign):
        return lax.ppermute(block, "blk", [(b, (b + (2 if b & 1 else -2) * sign) % 32) for b in range(32)])

    weight = kernel_table()
    constants = [jnp.asarray(table) for table in tables()]
    common = (group.reshape(1).astype(jnp.int32), weight, constants, [rows, *fields])

    crossed = cross(own)
    side = [beside(chunk, 1) for chunk in (own[: ROWS // 4], own[ROWS // 4 :])]
    other_side = jnp.concatenate([beside(chunk, -1) for chunk in (own[: ROWS // 4], own[ROWS // 4 :])], 0)
    total = stop(*common, [own])
    total = stop(*common, [crossed], total)
    total, side[1] = lax.optimization_barrier((total, side[1]))
    last = [cross(chunk) for chunk in side]
    same = jnp.where(((offset + low_z) & 1) == 0, jnp.concatenate(side, 0), other_side)
    total = stop(*common, [same], total)
    send, keep = stop(*common, last, total, True)

    near = everywhere(send, lambda g, b: (g ^ 1, b))
    far = everywhere(keep[1024:] + near[1024:], lambda g, b: (g ^ 2, b))
    result = -(keep[:1024] + near[:1024] + far)
    return result.reshape(512, 2, LANES).transpose(1, 0, 2).reshape(2, 65536)


def solution(mesh):
    in_specs = (P("blk", "grp"), P(("grp", "blk"), None), P(("grp", "blk")), P())
    out_specs = P("blk", "grp")
    return jax.shard_map(local, mesh=mesh, in_specs=in_specs, out_specs=out_specs, check_vma=False)
```

```python
import functools
import math

import jax
import jax.numpy as jnp
import numpy as np
from jax import lax
from jax.experimental import pallas as pl
from jax.experimental.pallas import tpu as pltpu
from jax.sharding import PartitionSpec as P

NG = 64
LANES = 128
ROWS = NG * NG
HALF = NG // 2
QUARTER = NG // 4
UNROLL = 32
FLOPS = 20_000_000_000
STRIDE = 72

box_length = 16.0
screen_square = 0.25
f32 = jnp.float32
bf16 = jnp.bfloat16


def two_terms(matrix):
    matrix = np.asarray(matrix, np.float32)
    high = matrix.astype(jnp.bfloat16)
    low = (matrix - high.astype(np.float32)).astype(jnp.bfloat16)
    return high, low


def tables():
    count = np.arange(NG)
    angle = 2.0 * np.pi * (count[:, None] * count[None, :] % NG) / NG
    h = np.cos(angle) + np.sin(angle)
    order = np.concatenate([np.arange(0, NG, 2), np.arange(1, NG, 2)])

    def left(matrix):
        high, low = two_terms(matrix)
        return np.concatenate([np.concatenate([high, high], 1), np.concatenate([low, low], 1)], 0)

    high, low = two_terms(np.kron(np.eye(2), h))
    right = np.concatenate([np.concatenate([high, low], 1)] * 2, 0)
    return left(h[:, order]), left(h), left(h[order, :]), right


def wave_square(index):
    signed = jnp.where(index < NG // 2, index, index - NG).astype(f32)
    wave = 2.0 * math.pi * signed / box_length
    return wave * wave


def split(value):
    high = value.astype(bf16)
    low = (value - high.astype(f32)).astype(bf16)
    return high, low


def left_product(table, value):
    high, low = split(value)
    out = jnp.dot(table, jnp.concatenate([high, low], 0), preferred_element_type=f32)
    return out[:NG] + out[NG:]


def right_product(value, table):
    high, low = split(value)
    out = jnp.dot(jnp.concatenate([high, low], 1), table, preferred_element_type=f32)
    return out[:, :LANES] + out[:, LANES:]


def swap_pairs(first, second):
    low = lax.broadcasted_iota(jnp.int32, first.shape, 1) < NG
    return (
        jnp.where(low, first, pltpu.roll(second, NG, 1)),
        jnp.where(low, pltpu.roll(first, NG, 1), second),
    )


def spread(row):
    turned = pltpu.roll(row, NG, 1)
    low = lax.broadcasted_iota(jnp.int32, row.shape, 1) < NG
    return jnp.concatenate([jnp.where(low, row, turned), jnp.where(low, turned, row)], 0)


def halves(value, index):
    return value[:, LANES * index : LANES * index + LANES]


TURNS = (0, 2, 1, 3)


def whole_rows(x, count):
    return pl.ds(pl.multiple_of(x * count, 8), count)


def write_kernel(weight):
    shape = (NG, LANES)
    at_x = wave_square(lax.broadcasted_iota(jnp.int32, shape, 0))
    at_z = wave_square(lax.broadcasted_iota(jnp.int32, shape, 1) & (NG - 1))
    for y in range(NG):
        wave = 2.0 * math.pi * (y if y < NG // 2 else y - NG) / box_length
        summed = at_x + at_z + wave * wave
        weight[y * NG : (y + 1) * NG, :] = 4.0 * math.pi / NG**3 / (summed + screen_square)


def stop_body(chunks, first, final, place, fwd_y, both_x, inv_y, both_z, *rest):
    row, rest = rest[:chunks], rest[chunks:]
    if chunks > 1:
        rest, whole = rest[:-1], rest[-1]
        size = ROWS // 2 // chunks
        for c in range(chunks):
            whole[c * size : (c + 1) * size, :] = row[c][...]
        row = whole
    else:
        row = row[0]
    fields, rest = rest[:4], rest[4:]
    if not first:
        (before, weight), rest = rest[:2], rest[2:]
    out, (one, two) = rest[:-2], rest[-2:]
    if first:
        weight = out[1]
        write_kernel(weight)

    def part(x):
        return spread(row[whole_rows(x, HALF), :])

    for turns in (TURNS[:2], TURNS[2:]):
        where = [(turn, u, (place[0] ^ turn) * QUARTER + u) for turn in turns for u in range(QUARTER)]
        products = []
        for turn, u, x in where:
            pair = swap_pairs(*[fields[turn][pl.ds(u * NG + t, HALF, 2), :] for t in range(2)])
            products.append(jnp.concatenate(pair, 0) * part(x))
        moved = [
            left_product(fwd_y[...], jnp.concatenate(products[i : i + 2], 1)) for i in range(0, len(where), 2)
        ]
        for i, (_, _, x) in enumerate(where):
            one[pl.ds(x, NG, STRIDE), :] = halves(moved[i // 2], i % 2)

    for start in range(0, NG, UNROLL):
        moved = []
        for k in range(start, start + UNROLL, 2):
            pair = jnp.concatenate([one[v * STRIDE : v * STRIDE + NG, :] for v in (k, k + 1)], 1)
            pair = left_product(both_x[...], pair)
            moved += [halves(pair, 0), halves(pair, 1)]
        plane = right_product(jnp.concatenate(moved, 0), both_z[...])
        plane = plane * weight[start * NG : (start + UNROLL) * NG, :]
        plane = right_product(plane, both_z[...])
        for u in range(0, UNROLL, 2):
            pair = jnp.concatenate([plane[v * NG : (v + 1) * NG] for v in (u, u + 1)], 1)
            pair = left_product(both_x[...], pair)
            for v in range(2):
                two[pl.ds(start + u + v, NG, STRIDE), :] = halves(pair, v)

    for step, turns in enumerate(((1, 3), (0, 2))):
        if final:
            where = [(place[0] ^ turn) * QUARTER + u for turn in turns for u in range(QUARTER)]
        else:
            where = list(range(step * HALF, (step + 1) * HALF))
        moved = []
        for i in range(0, HALF, 2):
            planes = [two[pl.ds(pl.multiple_of(x * STRIDE, 8), NG), :] for x in where[i : i + 2]]
            moved.append(left_product(inv_y[...], jnp.concatenate(planes, 1)))
        for i, x in enumerate(where):
            value = halves(moved[i // 2], i % 2) * part(x)
            if not first:
                value = value + before[whole_rows(x, NG), :]
            if final:
                for t, field in enumerate(swap_pairs(value[:HALF], value[HALF:])):
                    out[step][pl.ds(i * NG + t, HALF, 2), :] = field
            else:
                out[0][whole_rows(x, NG), :] = value


def stop(place, constants, fields, row, before=None, weight=None, final=False):
    vmem = pl.BlockSpec(memory_space=pltpu.VMEM)
    args = [place, *constants, *row, *fields] + ([] if before is None else [before, weight])
    half = jax.ShapeDtypeStruct((ROWS // 2, LANES), f32)
    whole = jax.ShapeDtypeStruct((ROWS, LANES), f32)
    return pl.pallas_call(
        functools.partial(stop_body, len(row), before is None, final),
        out_shape=(half, half) if final else (whole, whole) if before is None else whole,
        in_specs=[pl.BlockSpec(memory_space=pltpu.SMEM)] + [vmem] * (len(args) - 1),
        out_specs=(vmem, vmem) if final or before is None else vmem,
        scratch_shapes=[pltpu.VMEM((NG * STRIDE, LANES), f32)] * 2
        + [pltpu.VMEM((ROWS // 2, LANES), f32)] * (len(row) > 1),
        compiler_params=pltpu.CompilerParams(vmem_limit_bytes=16 * 2**20),
        cost_estimate=pl.CostEstimate(flops=FLOPS, bytes_accessed=9 * 2**20, transcendentals=0),
        name="stop",
    )(*args)


def scale_body(occupation, row, out):
    factor = jnp.sqrt(jnp.full((8, LANES), occupation[0], jnp.int32).astype(f32) * 0.5)
    for at in range(0, ROWS // 2, 8):
        out[at : at + 8, :] = row[at : at + 8, :] * factor


def moved(block, axes, route):
    return lax.ppermute(block, axes, route)


def everywhere(block, target):
    route = [(g * 32 + b, (lambda to: to[0] * 32 + to[1])(target(g, b))) for g in range(4) for b in range(32)]
    return lax.ppermute(block, ("grp", "blk"), route)


def pair_shift(block, distance):
    if distance % 16 == 0:
        return block
    return lax.ppermute(block, "blk", [(b, (b + 2 * distance) % 32) for b in range(32)])


def local(targets, sources, occupation, offsets):
    group = lax.axis_index("grp")
    low_z = lax.axis_index("blk") & 1

    rows = targets.reshape(2, 512, LANES).transpose(1, 0, 2).reshape(1024, LANES)
    fields = [everywhere(rows, lambda g, b, turn=turn: (g ^ turn, b)) for turn in (1, 2, 3)]

    scaled = pl.pallas_call(
        scale_body,
        out_shape=jax.ShapeDtypeStruct((ROWS // 2, LANES), f32),
        in_specs=[pl.BlockSpec(memory_space=pltpu.SMEM), pl.BlockSpec(memory_space=pltpu.VMEM)],
        name="scale",
    )(occupation, sources.reshape(ROWS // 2, LANES))
    offset = lax.dynamic_index_in_dim(offsets, group, 0, keepdims=False)
    own = lax.switch(
        (lax.shift_right_logical(offset, 1) + 1) & 15,
        [functools.partial(pair_shift, distance=d) for d in range(16)],
        scaled,
    )
    own, *fields = lax.optimization_barrier((own, *fields))

    def cross(block):
        return everywhere(block, lambda g, b: (g ^ 2 if g % 2 else g, b ^ 1))

    def beside(block, sign):
        return lax.ppermute(block, "blk", [(b, (b + (2 if b & 1 else -2) * sign) % 32) for b in range(32)])

    constants = [jnp.asarray(table) for table in tables()]
    common = (group.reshape(1).astype(jnp.int32), constants, [rows, *fields])

    crossed = cross(own)
    side = [beside(chunk, 1) for chunk in (own[: ROWS // 4], own[ROWS // 4 :])]
    other_side = jnp.concatenate([beside(chunk, -1) for chunk in (own[: ROWS // 4], own[ROWS // 4 :])], 0)
    total, weight = stop(*common, [own])
    total = stop(*common, [crossed], total, weight)
    total, side[1] = lax.optimization_barrier((total, side[1]))
    last = [cross(chunk) for chunk in side]
    same = jnp.where(((offset + low_z) & 1) == 0, jnp.concatenate(side, 0), other_side)
    total = stop(*common, [same], total, weight)
    send, keep = stop(*common, last, total, weight, True)

    near = everywhere(send, lambda g, b: (g ^ 1, b))
    far = everywhere(keep[1024:] + near[1024:], lambda g, b: (g ^ 2, b))
    result = -(keep[:1024] + near[:1024] + far)
    return result.reshape(512, 2, LANES).transpose(1, 0, 2).reshape(2, 65536)


def solution(mesh):
    in_specs = (P("blk", "grp"), P(("grp", "blk"), None), P(("grp", "blk")), P())
    out_specs = P("blk", "grp")
    return jax.shard_map(local, mesh=mesh, in_specs=in_specs, out_specs=out_specs, check_vma=False)
```

```python
import functools
import math

import jax
import jax.numpy as jnp
import numpy as np
from jax import lax
from jax.experimental import pallas as pl
from jax.experimental.pallas import tpu as pltpu
from jax.sharding import PartitionSpec as P

NG = 64
LANES = 128
ROWS = NG * NG
HALF = NG // 2
QUARTER = NG // 4
UNROLL = 32
CUT = 1280
FLOPS = 20_000_000_000
STRIDE = 72

box_length = 16.0
screen_square = 0.25
f32 = jnp.float32
bf16 = jnp.bfloat16


def two_terms(matrix):
    matrix = np.asarray(matrix, np.float32)
    high = matrix.astype(jnp.bfloat16)
    low = (matrix - high.astype(np.float32)).astype(jnp.bfloat16)
    return high, low


def tables():
    count = np.arange(NG)
    angle = 2.0 * np.pi * (count[:, None] * count[None, :] % NG) / NG
    h = np.cos(angle) + np.sin(angle)
    order = np.concatenate([np.arange(0, NG, 2), np.arange(1, NG, 2)])

    def left(matrix):
        high, low = two_terms(matrix)
        return np.concatenate([np.concatenate([high, high], 1), np.concatenate([low, low], 1)], 0)

    high, low = two_terms(np.kron(np.eye(2), h))
    right = np.concatenate([np.concatenate([high, low], 1)] * 2, 0)
    return left(h[:, order]), left(h), left(h[order, :]), right


def wave_square(index):
    signed = jnp.where(index < NG // 2, index, index - NG).astype(f32)
    wave = 2.0 * math.pi * signed / box_length
    return wave * wave


def split(value):
    high = value.astype(bf16)
    low = (value - high.astype(f32)).astype(bf16)
    return high, low


def left_product(table, value):
    high, low = split(value)
    out = jnp.dot(table, jnp.concatenate([high, low], 0), preferred_element_type=f32)
    return out[:NG] + out[NG:]


def right_product(value, table):
    high, low = split(value)
    out = jnp.dot(jnp.concatenate([high, low], 1), table, preferred_element_type=f32)
    return out[:, :LANES] + out[:, LANES:]


def swap_pairs(first, second):
    low = lax.broadcasted_iota(jnp.int32, first.shape, 1) < NG
    return (
        jnp.where(low, first, pltpu.roll(second, NG, 1)),
        jnp.where(low, pltpu.roll(first, NG, 1), second),
    )


def spread(row):
    turned = pltpu.roll(row, NG, 1)
    low = lax.broadcasted_iota(jnp.int32, row.shape, 1) < NG
    return jnp.concatenate([jnp.where(low, row, turned), jnp.where(low, turned, row)], 0)


def halves(value, index):
    return value[:, LANES * index : LANES * index + LANES]


TURNS = (0, 2, 1, 3)


def whole_rows(x, count):
    return pl.ds(pl.multiple_of(x * count, 8), count)


def write_kernel(weight):
    shape = (NG, LANES)
    at_x = wave_square(lax.broadcasted_iota(jnp.int32, shape, 0))
    at_z = wave_square(lax.broadcasted_iota(jnp.int32, shape, 1) & (NG - 1))
    for y in range(NG):
        wave = 2.0 * math.pi * (y if y < NG // 2 else y - NG) / box_length
        summed = at_x + at_z + wave * wave
        weight[y * NG : (y + 1) * NG, :] = 4.0 * math.pi / NG**3 / (summed + screen_square)


def stop_body(chunks, first, final, place, fwd_y, both_x, inv_y, both_z, *rest):
    row, rest = rest[:chunks], rest[chunks:]
    if chunks > 1:
        rest, whole = rest[:-1], rest[-1]
        begin = 0
        for chunk in row:
            whole[begin : begin + chunk.shape[0], :] = chunk[...]
            begin += chunk.shape[0]
        row = whole
    else:
        row = row[0]
    fields, rest = rest[:4], rest[4:]
    if not first:
        (before, weight), rest = rest[:2], rest[2:]
    out, (one, two) = rest[:-2], rest[-2:]
    if first:
        weight = out[1]
        write_kernel(weight)

    def part(x):
        return spread(row[whole_rows(x, HALF), :])

    for turns in (TURNS[:2], TURNS[2:]):
        where = [(turn, u, (place[0] ^ turn) * QUARTER + u) for turn in turns for u in range(QUARTER)]
        products = []
        for turn, u, x in where:
            pair = swap_pairs(*[fields[turn][pl.ds(u * NG + t, HALF, 2), :] for t in range(2)])
            products.append(jnp.concatenate(pair, 0) * part(x))
        moved = [
            left_product(fwd_y[...], jnp.concatenate(products[i : i + 2], 1)) for i in range(0, len(where), 2)
        ]
        for i, (_, _, x) in enumerate(where):
            one[pl.ds(x, NG, STRIDE), :] = halves(moved[i // 2], i % 2)

    for start in range(0, NG, UNROLL):
        moved = []
        for k in range(start, start + UNROLL, 2):
            pair = jnp.concatenate([one[v * STRIDE : v * STRIDE + NG, :] for v in (k, k + 1)], 1)
            pair = left_product(both_x[...], pair)
            moved += [halves(pair, 0), halves(pair, 1)]
        plane = right_product(jnp.concatenate(moved, 0), both_z[...])
        plane = plane * weight[start * NG : (start + UNROLL) * NG, :]
        plane = right_product(plane, both_z[...])
        for u in range(0, UNROLL, 2):
            pair = jnp.concatenate([plane[v * NG : (v + 1) * NG] for v in (u, u + 1)], 1)
            pair = left_product(both_x[...], pair)
            for v in range(2):
                two[pl.ds(start + u + v, NG, STRIDE), :] = halves(pair, v)

    for step, turns in enumerate(((1, 3), (0, 2))):
        if final:
            where = [(place[0] ^ turn) * QUARTER + u for turn in turns for u in range(QUARTER)]
        else:
            where = list(range(step * HALF, (step + 1) * HALF))
        moved = []
        for i in range(0, HALF, 2):
            planes = [two[pl.ds(pl.multiple_of(x * STRIDE, 8), NG), :] for x in where[i : i + 2]]
            moved.append(left_product(inv_y[...], jnp.concatenate(planes, 1)))
        for i, x in enumerate(where):
            value = halves(moved[i // 2], i % 2) * part(x)
            if not first:
                value = value + before[whole_rows(x, NG), :]
            if final:
                for t, field in enumerate(swap_pairs(value[:HALF], value[HALF:])):
                    out[step][pl.ds(i * NG + t, HALF, 2), :] = field
            else:
                out[0][whole_rows(x, NG), :] = value


def stop(place, constants, fields, row, before=None, weight=None, final=False):
    vmem = pl.BlockSpec(memory_space=pltpu.VMEM)
    args = [place, *constants, *row, *fields] + ([] if before is None else [before, weight])
    half = jax.ShapeDtypeStruct((ROWS // 2, LANES), f32)
    whole = jax.ShapeDtypeStruct((ROWS, LANES), f32)
    return pl.pallas_call(
        functools.partial(stop_body, len(row), before is None, final),
        out_shape=(half, half) if final else (whole, whole) if before is None else whole,
        in_specs=[pl.BlockSpec(memory_space=pltpu.SMEM)] + [vmem] * (len(args) - 1),
        out_specs=(vmem, vmem) if final or before is None else vmem,
        scratch_shapes=[pltpu.VMEM((NG * STRIDE, LANES), f32)] * 2
        + [pltpu.VMEM((ROWS // 2, LANES), f32)] * (len(row) > 1),
        compiler_params=pltpu.CompilerParams(vmem_limit_bytes=16 * 2**20),
        cost_estimate=pl.CostEstimate(flops=FLOPS, bytes_accessed=9 * 2**20, transcendentals=0),
        name="stop",
    )(*args)


def scale_body(occupation, row, out):
    factor = jnp.sqrt(jnp.full((8, LANES), occupation[0], jnp.int32).astype(f32) * 0.5)
    for at in range(0, ROWS // 2, 8):
        out[at : at + 8, :] = row[at : at + 8, :] * factor


def moved(block, axes, route):
    return lax.ppermute(block, axes, route)


def everywhere(block, target):
    route = [(g * 32 + b, (lambda to: to[0] * 32 + to[1])(target(g, b))) for g in range(4) for b in range(32)]
    return lax.ppermute(block, ("grp", "blk"), route)


def pair_shift(block, distance):
    if distance % 16 == 0:
        return block
    return lax.ppermute(block, "blk", [(b, (b + 2 * distance) % 32) for b in range(32)])


def local(targets, sources, occupation, offsets):
    group = lax.axis_index("grp")
    low_z = lax.axis_index("blk") & 1

    rows = targets.reshape(2, 512, LANES).transpose(1, 0, 2).reshape(1024, LANES)
    fields = [everywhere(rows, lambda g, b, turn=turn: (g ^ turn, b)) for turn in (1, 2, 3)]

    scaled = pl.pallas_call(
        scale_body,
        out_shape=jax.ShapeDtypeStruct((ROWS // 2, LANES), f32),
        in_specs=[pl.BlockSpec(memory_space=pltpu.SMEM), pl.BlockSpec(memory_space=pltpu.VMEM)],
        name="scale",
    )(occupation, sources.reshape(ROWS // 2, LANES))
    offset = lax.dynamic_index_in_dim(offsets, group, 0, keepdims=False)
    own = lax.switch(
        (lax.shift_right_logical(offset, 1) + 1) & 15,
        [functools.partial(pair_shift, distance=d) for d in range(16)],
        scaled,
    )
    own, *fields = lax.optimization_barrier((own, *fields))

    def cross(block):
        return everywhere(block, lambda g, b: (g ^ 2 if g % 2 else g, b ^ 1))

    def beside(block, sign):
        return lax.ppermute(block, "blk", [(b, (b + (2 if b & 1 else -2) * sign) % 32) for b in range(32)])

    constants = [jnp.asarray(table) for table in tables()]
    common = (group.reshape(1).astype(jnp.int32), constants, [rows, *fields])

    crossed = cross(own)
    side = [beside(chunk, 1) for chunk in (own[:CUT], own[CUT:])]
    other_side = jnp.concatenate([beside(chunk, -1) for chunk in (own[:CUT], own[CUT:])], 0)
    total, weight = stop(*common, [own])
    total = stop(*common, [crossed], total, weight)
    total, side[1] = lax.optimization_barrier((total, side[1]))
    last = [cross(chunk) for chunk in side]
    same = jnp.where(((offset + low_z) & 1) == 0, jnp.concatenate(side, 0), other_side)
    total = stop(*common, [same], total, weight)
    send, keep = stop(*common, last, total, weight, True)

    near = everywhere(send, lambda g, b: (g ^ 1, b))
    far = everywhere(keep[1024:] + near[1024:], lambda g, b: (g ^ 2, b))
    result = -(keep[:1024] + near[:1024] + far)
    return result.reshape(512, 2, LANES).transpose(1, 0, 2).reshape(2, 65536)


def solution(mesh):
    in_specs = (P("blk", "grp"), P(("grp", "blk"), None), P(("grp", "blk")), P())
    out_specs = P("blk", "grp")
    return jax.shard_map(local, mesh=mesh, in_specs=in_specs, out_specs=out_specs, check_vma=False)
```

```python
import functools
import math

import jax
import jax.numpy as jnp
import numpy as np
from jax import lax
from jax.experimental import pallas as pl
from jax.experimental.pallas import tpu as pltpu
from jax.sharding import PartitionSpec as P

NG = 64
LANES = 128
ROWS = NG * NG
HALF = NG // 2
QUARTER = NG // 4
UNROLL = 32
PLANES = 64
FLOPS = 20_000_000_000
STRIDE = 72

box_length = 16.0
screen_square = 0.25
f32 = jnp.float32
bf16 = jnp.bfloat16


def two_terms(matrix):
    matrix = np.asarray(matrix, np.float32)
    high = matrix.astype(jnp.bfloat16)
    low = (matrix - high.astype(np.float32)).astype(jnp.bfloat16)
    return high, low


def tables():
    count = np.arange(NG)
    angle = 2.0 * np.pi * (count[:, None] * count[None, :] % NG) / NG
    h = np.cos(angle) + np.sin(angle)
    order = np.concatenate([np.arange(0, NG, 2), np.arange(1, NG, 2)])

    def left(matrix):
        high, low = two_terms(matrix)
        return np.concatenate([np.concatenate([high, high], 1), np.concatenate([low, low], 1)], 0)

    high, low = two_terms(np.kron(np.eye(2), h))
    right = np.concatenate([np.concatenate([high, low], 1)] * 2, 0)
    return left(h[:, order]), left(h), left(h[order, :]), right


def wave_square(index):
    signed = jnp.where(index < NG // 2, index, index - NG).astype(f32)
    wave = 2.0 * math.pi * signed / box_length
    return wave * wave


def split(value):
    high = value.astype(bf16)
    low = (value - high.astype(f32)).astype(bf16)
    return high, low


def left_product(table, value):
    high, low = split(value)
    out = jnp.dot(table, jnp.concatenate([high, low], 0), preferred_element_type=f32)
    return out[:NG] + out[NG:]


def right_product(value, table):
    high, low = split(value)
    out = jnp.dot(jnp.concatenate([high, low], 1), table, preferred_element_type=f32)
    return out[:, :LANES] + out[:, LANES:]


def swap_pairs(first, second):
    low = lax.broadcasted_iota(jnp.int32, first.shape, 1) < NG
    return (
        jnp.where(low, first, pltpu.roll(second, NG, 1)),
        jnp.where(low, pltpu.roll(first, NG, 1), second),
    )


def spread(row):
    turned = pltpu.roll(row, NG, 1)
    low = lax.broadcasted_iota(jnp.int32, row.shape, 1) < NG
    return jnp.concatenate([jnp.where(low, row, turned), jnp.where(low, turned, row)], 0)


def halves(value, index):
    return value[:, LANES * index : LANES * index + LANES]


TURNS = (0, 2, 1, 3)


def whole_rows(x, count):
    return pl.ds(pl.multiple_of(x * count, 8), count)


def write_kernel(weight):
    shape = (NG, LANES)
    at_x = wave_square(lax.broadcasted_iota(jnp.int32, shape, 0))
    at_z = wave_square(lax.broadcasted_iota(jnp.int32, shape, 1) & (NG - 1))
    for y in range(NG):
        wave = 2.0 * math.pi * (y if y < NG // 2 else y - NG) / box_length
        summed = at_x + at_z + wave * wave
        weight[y * NG : (y + 1) * NG, :] = 4.0 * math.pi / NG**3 / (summed + screen_square)


def stop_body(chunks, first, final, place, fwd_y, both_x, inv_y, both_z, *rest):
    row, rest = rest[:chunks], rest[chunks:]
    if chunks > 1:
        rest, whole = rest[:-1], rest[-1]
        size = ROWS // 2 // chunks
        for c in range(chunks):
            whole[c * size : (c + 1) * size, :] = row[c][...]
        row = whole
    else:
        row = row[0]
    fields, rest = rest[:4], rest[4:]
    if not first:
        (before, weight), rest = rest[:2], rest[2:]
    out, (one, two) = rest[:-2], rest[-2:]
    if first:
        weight = out[1]
        write_kernel(weight)

    def part(x):
        return spread(row[whole_rows(x, HALF), :])

    for turns in (TURNS[:2], TURNS[2:]):
        where = [(turn, u, (place[0] ^ turn) * QUARTER + u) for turn in turns for u in range(QUARTER)]
        products = []
        for turn, u, x in where:
            pair = swap_pairs(*[fields[turn][pl.ds(u * NG + t, HALF, 2), :] for t in range(2)])
            products.append(jnp.concatenate(pair, 0) * part(x))
        moved = [
            left_product(fwd_y[...], jnp.concatenate(products[i : i + 2], 1)) for i in range(0, len(where), 2)
        ]
        for i, (_, _, x) in enumerate(where):
            one[pl.ds(x, NG, STRIDE), :] = halves(moved[i // 2], i % 2)

    for start in range(0, NG, PLANES):
        moved = []
        for k in range(start, start + PLANES, 2):
            pair = jnp.concatenate([one[v * STRIDE : v * STRIDE + NG, :] for v in (k, k + 1)], 1)
            pair = left_product(both_x[...], pair)
            moved += [halves(pair, 0), halves(pair, 1)]
        plane = right_product(jnp.concatenate(moved, 0), both_z[...])
        plane = plane * weight[start * NG : (start + PLANES) * NG, :]
        plane = right_product(plane, both_z[...])
        for u in range(0, PLANES, 2):
            pair = jnp.concatenate([plane[v * NG : (v + 1) * NG] for v in (u, u + 1)], 1)
            pair = left_product(both_x[...], pair)
            for v in range(2):
                two[pl.ds(start + u + v, NG, STRIDE), :] = halves(pair, v)

    for step, turns in enumerate(((1, 3), (0, 2))):
        if final:
            where = [(place[0] ^ turn) * QUARTER + u for turn in turns for u in range(QUARTER)]
        else:
            where = list(range(step * HALF, (step + 1) * HALF))
        moved = []
        for i in range(0, HALF, 2):
            planes = [two[pl.ds(pl.multiple_of(x * STRIDE, 8), NG), :] for x in where[i : i + 2]]
            moved.append(left_product(inv_y[...], jnp.concatenate(planes, 1)))
        for i, x in enumerate(where):
            value = halves(moved[i // 2], i % 2) * part(x)
            if not first:
                value = value + before[whole_rows(x, NG), :]
            if final:
                for t, field in enumerate(swap_pairs(value[:HALF], value[HALF:])):
                    out[step][pl.ds(i * NG + t, HALF, 2), :] = field
            else:
                out[0][whole_rows(x, NG), :] = value


def stop(place, constants, fields, row, before=None, weight=None, final=False):
    vmem = pl.BlockSpec(memory_space=pltpu.VMEM)
    args = [place, *constants, *row, *fields] + ([] if before is None else [before, weight])
    half = jax.ShapeDtypeStruct((ROWS // 2, LANES), f32)
    whole = jax.ShapeDtypeStruct((ROWS, LANES), f32)
    return pl.pallas_call(
        functools.partial(stop_body, len(row), before is None, final),
        out_shape=(half, half) if final else (whole, whole) if before is None else whole,
        in_specs=[pl.BlockSpec(memory_space=pltpu.SMEM)] + [vmem] * (len(args) - 1),
        out_specs=(vmem, vmem) if final or before is None else vmem,
        scratch_shapes=[pltpu.VMEM((NG * STRIDE, LANES), f32)] * 2
        + [pltpu.VMEM((ROWS // 2, LANES), f32)] * (len(row) > 1),
        compiler_params=pltpu.CompilerParams(vmem_limit_bytes=16 * 2**20),
        cost_estimate=pl.CostEstimate(flops=FLOPS, bytes_accessed=9 * 2**20, transcendentals=0),
        name="stop",
    )(*args)


def scale_body(occupation, row, out):
    factor = jnp.sqrt(jnp.full((8, LANES), occupation[0], jnp.int32).astype(f32) * 0.5)
    for at in range(0, ROWS // 2, 8):
        out[at : at + 8, :] = row[at : at + 8, :] * factor


def moved(block, axes, route):
    return lax.ppermute(block, axes, route)


def everywhere(block, target):
    route = [(g * 32 + b, (lambda to: to[0] * 32 + to[1])(target(g, b))) for g in range(4) for b in range(32)]
    return lax.ppermute(block, ("grp", "blk"), route)


def pair_shift(block, distance):
    if distance % 16 == 0:
        return block
    return lax.ppermute(block, "blk", [(b, (b + 2 * distance) % 32) for b in range(32)])


def local(targets, sources, occupation, offsets):
    group = lax.axis_index("grp")
    low_z = lax.axis_index("blk") & 1

    rows = targets.reshape(2, 512, LANES).transpose(1, 0, 2).reshape(1024, LANES)
    fields = [everywhere(rows, lambda g, b, turn=turn: (g ^ turn, b)) for turn in (1, 2, 3)]

    scaled = pl.pallas_call(
        scale_body,
        out_shape=jax.ShapeDtypeStruct((ROWS // 2, LANES), f32),
        in_specs=[pl.BlockSpec(memory_space=pltpu.SMEM), pl.BlockSpec(memory_space=pltpu.VMEM)],
        name="scale",
    )(occupation, sources.reshape(ROWS // 2, LANES))
    offset = lax.dynamic_index_in_dim(offsets, group, 0, keepdims=False)
    own = lax.switch(
        (lax.shift_right_logical(offset, 1) + 1) & 15,
        [functools.partial(pair_shift, distance=d) for d in range(16)],
        scaled,
    )
    own, *fields = lax.optimization_barrier((own, *fields))

    def cross(block):
        return everywhere(block, lambda g, b: (g ^ 2 if g % 2 else g, b ^ 1))

    def beside(block, sign):
        return lax.ppermute(block, "blk", [(b, (b + (2 if b & 1 else -2) * sign) % 32) for b in range(32)])

    constants = [jnp.asarray(table) for table in tables()]
    common = (group.reshape(1).astype(jnp.int32), constants, [rows, *fields])

    crossed = cross(own)
    side = [beside(chunk, 1) for chunk in (own[: ROWS // 4], own[ROWS // 4 :])]
    other_side = jnp.concatenate([beside(chunk, -1) for chunk in (own[: ROWS // 4], own[ROWS // 4 :])], 0)
    total, weight = stop(*common, [own])
    total = stop(*common, [crossed], total, weight)
    total, side[1] = lax.optimization_barrier((total, side[1]))
    last = [cross(chunk) for chunk in side]
    same = jnp.where(((offset + low_z) & 1) == 0, jnp.concatenate(side, 0), other_side)
    total = stop(*common, [same], total, weight)
    send, keep = stop(*common, last, total, weight, True)

    near = everywhere(send, lambda g, b: (g ^ 1, b))
    far = everywhere(keep[1024:] + near[1024:], lambda g, b: (g ^ 2, b))
    result = -(keep[:1024] + near[:1024] + far)
    return result.reshape(512, 2, LANES).transpose(1, 0, 2).reshape(2, 65536)


def solution(mesh):
    in_specs = (P("blk", "grp"), P(("grp", "blk"), None), P(("grp", "blk")), P())
    out_specs = P("blk", "grp")
    return jax.shard_map(local, mesh=mesh, in_specs=in_specs, out_specs=out_specs, check_vma=False)
```
